32 devices in a mesh: aux: 4 (over x, core), cd: 4 (over z), ab: 2 (over y).
Axes of the slice: x: 2, y: 2, z: 4, core: 2. Of those that a mesh axis runs over, the one named last changes fastest.
Arguments:
- left_integrals: bfloat16 [4, 2048, 2048], P('cd', 'ab', 'aux'), may hold values from -6 to 6
- right_integrals: bfloat16 [2, 2048, 2048], P('ab', 'cd', 'aux'), may hold values from -6 to 6
- metric_factor: bfloat16 [2048, 2048], P('aux'), may hold values from -0.125 to 0.125
- amplitudes: bfloat16 [32, 2048, 2048], P(None, 'ab', 'cd'), may hold values from -6.4373016e-05 to 6.4373016e-05
- tile_sizes: int32 [16], replicated, may hold values from 1 to 256, 2048 in all
- pair_mask: int32 [16, 16], replicated, may hold values 0 or 1
Outputs:
- ladder_residual: float32 [4, 2, 32], P('cd', 'ab')
The draws below stay inside these ranges and needn't reach their ends.
Inputs may be any that keep to these rules, and one draw needn't show every extreme that they name: `tile_sizes`: the 16 tile sizes sum to 2048.
All inputs are finite; a program needn't handle non-finite values.
Results may differ from the reference program's by a relative error of at most 0.0038.
Values may be sent and summed in bfloat16 or wider, within the bound.
A program may use at most 128 MiB of HBM per device.

```python
import math
import jax
import jax.numpy as jnp
import numpy as np
from jax import lax

NVIR = 2048
NAUX = 2048
NPAIR = 32
NTILE = 16
TILE_MOST = 256
AUX_BLOCKS = 4
A_WIN = 4
B_WIN = 2


def plant(values, own_key, smallest, high):
    place = [jax.random.randint(jax.random.fold_in(own_key, axis), (), 0, length) for axis, length in enumerate(values.shape)]
    longest = values.shape.index(max(values.shape))
    beside = place[:longest] + [(place[longest] + 1) % values.shape[longest]] + place[longest + 1:]
    return values.at[tuple(place)].set(smallest).at[tuple(beside)].set(high)


def level_of(own_key, shape, split, smallest, top_value):
    factor_of = 1.0
    for axis_at, blocks in split:
        draws = jax.random.uniform(jax.random.fold_in(jax.random.fold_in(own_key, 6), axis_at), (blocks,), jnp.float32, smallest / len(split), top_value / len(split))
        factor_of = factor_of * jnp.repeat(jnp.exp(draws), shape[axis_at] // blocks).reshape((-1,) + (1,) * (len(shape) - 1 - axis_at))
    return factor_of


def profile(number_of, total, most, lean):
    loads = [(1 << 20) // math.isqrt(rank ** lean) + 1 for rank in range(2, number_of + 1)]
    rest, counts = total - most - (number_of - 1), [1] * (number_of - 1)
    while rest > 0:
        movable = [i for i in range(number_of - 1) if counts[i] < most]
        whole, left = sum([loads[i] for i in movable]), rest
        for i in movable:
            addition = min(most - counts[i], max(1, left * loads[i] // whole), rest)
            counts[i] = counts[i] + addition
            rest = rest - addition
    return np.array([most] + counts)


def uneven_parts(own_key, number_of, total, limit, slope):
    if number_of == 2:
        one = jax.random.randint(own_key, (), max(1, total - limit), min(limit, total - 1) + 1)
        return jnp.stack([one, total - one])
    lengths = jnp.asarray(profile(number_of, total, limit, slope), jnp.int32)
    twos = (number_of - 1) // 2
    source_of, taker = lengths[1:1 + 2 * twos:2], lengths[2:2 + 2 * twos:2]
    room = jnp.minimum(source_of - 1, limit - taker)
    moved = jax.random.randint(jax.random.fold_in(own_key, 1), (twos,), 0, 1 << 20) % (room + 1)
    lengths = lengths.at[1:1 + 2 * twos:2].set(source_of - moved).at[2:2 + 2 * twos:2].set(taker + moved)
    return lengths[jax.random.permutation(jax.random.fold_in(own_key, 2), number_of)]


def gaussian(key, extent, scale, bound, pieces=(), held_as=jnp.bfloat16):
    drawn = jax.random.normal(key, extent, jnp.float32) * scale
    if len(pieces) > 0:
        drawn = level_of(key, extent, pieces, -0.22, 0.18) * drawn
    return jnp.clip(drawn, min=-bound, max=bound).astype(held_as)


def setup_inputs(seed: int = 0) -> dict:
    key_of = jax.random.split(jax.random.key(seed), 7)
    left_integrals = gaussian(key_of[0], (A_WIN, NVIR, NAUX), 1.0, 6.0, ((0, 4), (1, 2), (2, 4)))
    right_integrals = gaussian(key_of[1], (B_WIN, NVIR, NAUX), 1.0, 6.0, ((0, 2), (1, 4), (2, 4)))
    metric_factor = gaussian(key_of[2], (NAUX, NAUX), NAUX ** -0.5, 0.125, ((0, 4),))
    amplitudes = gaussian(key_of[3], (NPAIR, NVIR, NVIR), (1.0 / (NVIR * NAUX ** 0.5)), 6.437301635742188e-05, ((1, 2), (2, 4)))
    tile_sizes = uneven_parts(key_of[4], NTILE, NVIR, TILE_MOST, 2).astype(jnp.int32)
    pair_mask = plant((jax.random.randint(key_of[5], (NTILE, NTILE), 0, 2) < 1).astype(jnp.int32), jax.random.fold_in(key_of[5], 1), 0, 1)
    return {"left_integrals": left_integrals, "right_integrals": right_integrals, "metric_factor": metric_factor, "amplitudes": amplitudes, "tile_sizes": tile_sizes, "pair_mask": pair_mask}


def tile_numbers(tile_sizes):
    tile_end = jnp.cumsum(tile_sizes).astype(jnp.int32)
    positions = jnp.arange(NVIR, dtype=jnp.int32)
    return jnp.sum((positions[:, None] >= tile_end[None, :]).astype(jnp.int32), axis=1).astype(jnp.int32)


def reference(left_integrals, right_integrals, metric_factor, amplitudes, tile_sizes, pair_mask):
    tiles = tile_numbers(tile_sizes)
    keep_mask = pair_mask[tiles[:, None], tiles[None, :]]
    kept = amplitudes * keep_mask.astype(jnp.bfloat16)
    kept_wide = kept.astype(jnp.float32)
    left_fit = jnp.einsum("acp,pq->qac", left_integrals.astype(jnp.float32), metric_factor.astype(jnp.float32),
                          precision=lax.Precision.HIGHEST).astype(jnp.bfloat16)
    right_fit = jnp.einsum("bdp,pq->qbd", right_integrals.astype(jnp.float32), metric_factor.astype(jnp.float32),
                           precision=lax.Precision.HIGHEST).astype(jnp.bfloat16)
    block_width = NAUX // AUX_BLOCKS
    right_flat = right_fit.reshape(NAUX, B_WIN * NVIR)

    def one_virtual(left_slab):
        total = jnp.zeros((B_WIN, NPAIR), jnp.float32)
        for group in range(AUX_BLOCKS):
            lower = group * block_width
            ladder = jnp.dot(left_slab[lower:lower + block_width].T, right_flat[lower:lower + block_width],
                             preferred_element_type=jnp.float32).astype(jnp.bfloat16)
            ladder_wide = ladder.reshape(NVIR, B_WIN, NVIR).astype(jnp.float32)
            total = total + jnp.einsum("cbd,icd->bi", ladder_wide, kept_wide, precision=lax.Precision.HIGHEST)
        return total

    return lax.map(one_virtual, jnp.transpose(left_fit, (1, 0, 2)))
```

```python
import functools

import jax
import jax.numpy as jnp
from jax import lax
from jax.experimental import pallas as pl
from jax.experimental.pallas import tpu as pltpu
from jax.sharding import PartitionSpec as P

NT = (((1,), (1,)), ((), ()))
NN = (((1,), (0,)), ((), ()))
GROUP = 16
MESH = pl.DeviceIdType.MESH


def dot(x, y, dims):
    return lax.dot_general(x, y, dims, preferred_element_type=jnp.float32)


def kernel(A, Z, B, CB, sizes, left, right, metric, pair, amp, out,
           gathered, send1, got1, own, chip, got2, t_hi, t_lo, fit, amps, ladder, acc,
           hot_rows, hot_cols, part, got_z, mine, got_ab,
           z_send, z_recv, s_send, s_recv, x_send, x_recv, t_send, t_recv,
           u_send, u_recv, amp_sem, own_sem, fz_send, fz_recv, fa_send, fa_recv):
    aux, z, y = lax.axis_index("aux"), lax.axis_index("cd"), lax.axis_index("ab")
    C, PW = left.shape
    D = right.shape[0]
    Q = metric.shape[1]
    I = amp.shape[0]
    T = pair.shape[0]
    NC = C // CB
    H = D // 2
    QB = min(512, Q)
    core = lax.rem(aux, 2)
    sibling = aux + 1 - 2 * core

    def rcopy(src, dst, ss, rs, dev):
        return pltpu.make_async_remote_copy(src_ref=src, dst_ref=dst, send_sem=ss, recv_sem=rs,
                                            device_id=dev, device_id_type=MESH)

    def plane_peer(o):
        flat = lax.rem(aux * B + y + o, A * B)
        return {"aux": flat // B, "ab": lax.rem(flat, B)}

    def amp_copy(k, slot):
        rows = pl.ds(pl.multiple_of(k * CB, CB), CB)
        return pltpu.make_async_copy(amp.at[:, rows, :], amps.at[slot], amp_sem.at[slot])

    barrier = pltpu.get_barrier_semaphore()
    for o in range(1, Z):
        pl.semaphore_signal(barrier, inc=1, device_id={"cd": lax.rem(z + o, Z)}, device_id_type=MESH)
    for o in range(1, A * B):
        pl.semaphore_signal(barrier, inc=1, device_id=plane_peer(o), device_id_type=MESH)
    pl.semaphore_wait(barrier, Z - 1 + A * B - 1)

    def chunk(k):
        return pl.ds(pl.multiple_of(k * CB, CB), CB)

    def push(src, o, k, way):
        dev = {"cd": z + 1} if way == 0 else {"cd": z - 1}
        return rcopy(src, gathered.at[o, chunk(k)], z_send.at[way, o, k], z_recv.at[o, k], dev)

    def first(k, c):
        @pl.when(z < Z - 1)
        def _():
            push(left.at[chunk(k)], z, k, 0).start()

        @pl.when(z > 0)
        def _():
            push(left.at[chunk(k)], z, k, 1).start()
        return c

    lax.fori_loop(0, NC, first, 0)
    own_copy = pltpu.make_async_copy(left, gathered.at[z], own_sem)
    own_copy.start()
    amp_copy(0, 0).start()
    if NC > 1:
        amp_copy(1, 1).start()

    def relay_chunk(h, k):
        @pl.when(z - h >= 0)
        def _():
            o = z - h
            push(gathered.at[o, chunk(k)], o, k, 0).wait_recv()
            if h < Z - 1:
                @pl.when(z < Z - 1)
                def _():
                    push(gathered.at[o, chunk(k)], o, k, 0).start()

        @pl.when(z + h < Z)
        def _():
            o = z + h
            push(gathered.at[o, chunk(k)], o, k, 1).wait_recv()
            if h < Z - 1:
                @pl.when(z > 0)
                def _():
                    push(gathered.at[o, chunk(k)], o, k, 1).start()

    def relay(h):
        def step(k, c):
            relay_chunk(h, k)
            return c
        lax.fori_loop(0, NC, step, 0)

    mine_rows = pl.ds(pl.multiple_of(core * H, H), H)
    other_rows = pl.ds(pl.multiple_of((1 - core) * H, H), H)

    def cols(j):
        return pl.ds(pl.multiple_of(j * QB, QB), QB)

    def fit_other(j, c):
        send1[:, cols(j)] = dot(right[other_rows, :], metric[:, cols(j)], NN).astype(jnp.bfloat16)
        return c

    lax.fori_loop(0, Q // QB, fit_other, 0)
    pair_copy = rcopy(send1, got1, s_send, s_recv, {"aux": sibling})
    pair_copy.start()

    def fit_own(j, c):
        own[:, cols(j)] = dot(right[mine_rows, :], metric[:, cols(j)], NN)
        return c

    lax.fori_loop(0, Q // QB, fit_own, 0)
    pair_copy.wait()

    def add_pair(j, c):
        total = own[:, cols(j)] + got1[:, cols(j)].astype(jnp.float32)
        own[:, cols(j)] = total
        chip[:, cols(j)] = total.astype(jnp.bfloat16)
        return c

    lax.fori_loop(0, Q // QB, add_pair, 0)
    x_copies = [rcopy(chip, got2.at[n], x_send.at[n], x_recv.at[n], {"aux": lax.rem(aux + 2 * n + 2, A)})
                for n in range(A // 2 - 1)]
    for cp in x_copies:
        cp.start()

    rows_at = y * C + lax.broadcasted_iota(jnp.int32, (C, T), 0)
    rows_tile = lax.broadcasted_iota(jnp.int32, (C, T), 1)
    cols_at = z * D + lax.broadcasted_iota(jnp.int32, (T, D), 1)
    cols_tile = lax.broadcasted_iota(jnp.int32, (T, D), 0)
    row_hot = jnp.zeros((C, T), jnp.float32)
    col_hot = jnp.zeros((T, D), jnp.float32)
    low = jnp.int32(0)
    for t in range(T):
        high = low + sizes[t]
        row_hot = jnp.where((rows_tile == t) & (rows_at >= low) & (rows_at < high), 1.0, row_hot)
        col_hot = jnp.where((cols_tile == t) & (cols_at >= low) & (cols_at < high), 1.0, col_hot)
        low = high
    pair_bf = pair[...].astype(jnp.float32).astype(jnp.bfloat16)
    hot_rows[...] = dot(row_hot.astype(jnp.bfloat16), pair_bf, NN).astype(jnp.bfloat16)
    hot_cols[...] = col_hot.astype(jnp.bfloat16)
    acc[...] = jnp.zeros_like(acc)
    part[...] = jnp.zeros_like(part)

    if Z > 2:
        relay(1)

    for cp in x_copies:
        cp.wait()

    def total_t(j, c):
        total = own[:, cols(j)]
        for n in range(A // 2 - 1):
            total = total + got2[n, :, cols(j)].astype(jnp.float32)
        hi = total.astype(jnp.bfloat16)
        t_hi[mine_rows, cols(j)] = hi
        t_lo[mine_rows, cols(j)] = (total - hi.astype(jnp.float32)).astype(jnp.bfloat16)
        return c

    lax.fori_loop(0, Q // QB, total_t, 0)
    t_copies = [rcopy(ref.at[mine_rows], ref.at[mine_rows], t_send.at[n], t_recv.at[n], {"aux": sibling})
                for n, ref in enumerate((t_hi, t_lo))]
    for cp in t_copies:
        cp.start()

    def back(half):
        def step(j, c):
            keys = pl.ds(pl.multiple_of(j * 256, 256), 256)
            fit[y, half, keys] = (dot(t_hi[half, :], metric[keys, :], NT)
                                  + dot(t_lo[half, :], metric[keys, :], NT)).astype(jnp.bfloat16)
            return c
        lax.fori_loop(0, PW // 256, step, 0)

    back(mine_rows)
    for cp in t_copies:
        cp.wait()
    back(other_rows)

    def u_copy(o):
        return rcopy(fit.at[y], fit.at[y], u_send.at[o - 1], u_recv.at[o - 1], {"ab": lax.rem(y + o, B)})

    for o in range(1, B):
        u_copy(o).start()
    for h in range(2, Z - 1):
        relay(h)
    own_copy.wait()
    for o in range(1, B):
        src = lax.rem(y - o + B, B)
        rcopy(fit.at[src], fit.at[src], u_send.at[o - 1], u_recv.at[o - 1], {"ab": lax.rem(y + o, B)}).wait_recv()
        u_copy(o).wait_send()

    NR = B * 2 * Z * GROUP
    NG = CB // GROUP
    NB = min(NR, 256)

    def ladder_chunk(k, carry):
        slot = lax.rem(k, 2)
        relay_chunk(Z - 1, k)
        lefts = gathered[:, chunk(k), :].reshape(Z * CB, PW)
        keep = dot(hot_rows[chunk(k), :], hot_cols[...], NN)
        for b in range(B):
            terms = dot(lefts, fit[b], NT).reshape(Z, CB, D) * keep[None]
            hi = terms.astype(jnp.bfloat16)
            lo = (terms - hi.astype(jnp.float32)).astype(jnp.bfloat16)
            for g in range(NG):
                ladder[g, b, 0] = hi[:, g * GROUP:(g + 1) * GROUP, :]
                ladder[g, b, 1] = lo[:, g * GROUP:(g + 1) * GROUP, :]
        amp_copy(k, slot).wait()

        def contract(g, c):
            kept = amps[slot, :, pl.ds(pl.multiple_of(g * GROUP, GROUP), GROUP), :].reshape(I * GROUP, D)
            flat = ladder[g].reshape(NR, D)
            for n in range(0, NR, NB):
                acc[:, n:n + NB] += dot(kept, flat[n:n + NB], NT)
            return c

        lax.fori_loop(0, NG, contract, 0)

        @pl.when(k + 2 < NC)
        def _():
            amp_copy(k + 2, slot).start()
        return carry

    lax.fori_loop(0, NC, ladder_chunk, 0)

    total = acc[...]
    same = (lax.rem(lax.broadcasted_iota(jnp.int32, total.shape, 0), GROUP)
            == lax.rem(lax.broadcasted_iota(jnp.int32, total.shape, 1), GROUP))
    total = jnp.sum(jnp.where(same, total, 0.0).reshape(I, GROUP, NR), axis=1)
    pick_row = lax.broadcasted_iota(jnp.int32, (Z * 8, NR), 0)
    pick_col = lax.broadcasted_iota(jnp.int32, (Z * 8, NR), 1)
    want = lax.rem(lax.div(pick_col, GROUP), Z) * 8 + lax.div(pick_col, 2 * Z * GROUP)
    pick = jnp.where(pick_row == want, 1.0, 0.0)
    sums = lax.dot_general(pick, total, NT, precision=lax.Precision.HIGHEST,
                           preferred_element_type=jnp.float32)
    part[:, :, :I] = sums.reshape(Z, 8, I)

    def fz(o):
        dest = lax.rem(z + o, Z)
        return rcopy(part.at[dest], got_z.at[o - 1], fz_send.at[o - 1], fz_recv.at[o - 1], {"cd": dest})

    for o in range(1, Z):
        fz(o).start()
    summed = part[z]
    for o in range(1, Z):
        fz(o).wait()
        summed = summed + got_z[o - 1]
    mine[...] = summed

    def fa(o):
        return rcopy(mine, got_ab.at[o - 1], fa_send.at[o - 1], fa_recv.at[o - 1], plane_peer(o))

    for o in range(1, A * B):
        fa(o).start()
    for o in range(1, A * B):
        fa(o).wait()
        summed = summed + got_ab[o - 1]
    row = lax.broadcasted_iota(jnp.int32, summed.shape, 0)
    out[...] = jnp.sum(jnp.where(row == y, summed, 0.0), axis=0, keepdims=True)[:, :I]

    for h in range(0, Z - 1):
        for way in (0, 1):
            o = z - h if way == 0 else z + h
            ok = (z - h >= 0) & (z < Z - 1) if way == 0 else (z + h < Z) & (z > 0)

            def drain(k, c, o=o, way=way, ok=ok):
                @pl.when(ok)
                def _():
                    push(gathered.at[o, chunk(k)], o, k, way).wait_send()
                return c
            lax.fori_loop(0, NC, drain, 0)


def body(left, right, metric, amplitudes, sizes, pair):
    A, Z, B = lax.axis_size("aux"), lax.axis_size("cd"), lax.axis_size("ab")
    a_local, C, PW = left.shape
    b_local, D, _ = right.shape
    Q = metric.shape[1]
    I = amplitudes.shape[0]
    T = pair.shape[0]
    CB = min(128, C)
    NC = C // CB
    H = D // 2
    NR = B * 2 * Z * GROUP
    X = max(A // 2 - 1, 1)
    bf, f32 = jnp.bfloat16, jnp.float32
    dma = pltpu.SemaphoreType.DMA
    vmem = pl.BlockSpec(memory_space=pltpu.VMEM)
    out = pl.pallas_call(
        functools.partial(kernel, A, Z, B, CB),
        out_shape=jax.ShapeDtypeStruct((1, I), f32),
        in_specs=[pl.BlockSpec(memory_space=pltpu.SMEM), vmem, vmem, vmem, vmem,
                  pl.BlockSpec(memory_space=pl.ANY)],
        out_specs=vmem,
        scratch_shapes=[
            pltpu.VMEM((Z, C, PW), bf),
            pltpu.VMEM((H, Q), bf), pltpu.VMEM((H, Q), bf), pltpu.VMEM((H, Q), f32),
            pltpu.VMEM((H, Q), bf), pltpu.VMEM((X, H, Q), bf),
            pltpu.VMEM((D, Q), bf), pltpu.VMEM((D, Q), bf),
            pltpu.VMEM((B, D, PW), bf),
            pltpu.VMEM((2, I, CB, D), bf),
            pltpu.VMEM((CB // GROUP, B, 2, Z, GROUP, D), bf),
            pltpu.VMEM((I * GROUP, NR), f32),
            pltpu.VMEM((C, T), bf), pltpu.VMEM((T, D), bf),
            pltpu.VMEM((Z, 8, 128), f32), pltpu.VMEM((max(Z - 1, 1), 8, 128), f32),
            pltpu.VMEM((8, 128), f32), pltpu.VMEM((max(A * B - 1, 1), 8, 128), f32),
            dma((2, Z, NC)), dma((Z, NC)), dma, dma, dma((X,)), dma((X,)), dma((2,)), dma((2,)),
            dma((max(B - 1, 1),)), dma((max(B - 1, 1),)), dma((2,)), dma,
            dma((max(Z - 1, 1),)), dma((max(Z - 1, 1),)),
            dma((max(A * B - 1, 1),)), dma((max(A * B - 1, 1),)),
        ],
        compiler_params=pltpu.CompilerParams(collective_id=0, has_side_effects=True,
                                             vmem_limit_bytes=60 * 1024 * 1024),
        name="ladder",
    )(sizes, left.reshape(C, PW), right.reshape(D, PW), metric, pair, amplitudes)
    return out.reshape(a_local, b_local, I)


def solution(mesh):
    return jax.shard_map(
        body,
        mesh=mesh,
        in_specs=(
            P("cd", "ab", "aux"),
            P("ab", "cd", "aux"),
            P("aux", None),
            P(None, "ab", "cd"),
            P(),
            P(),
        ),
        out_specs=P("cd", "ab", None),
        check_vma=False,
    )
```

```python
import functools

import jax
import jax.numpy as jnp
from jax import lax
from jax.experimental import pallas as pl
from jax.experimental.pallas import tpu as pltpu
from jax.sharding import PartitionSpec as P

NT = (((1,), (1,)), ((), ()))
NN = (((1,), (0,)), ((), ()))
GROUP = 16
MESH = pl.DeviceIdType.MESH


def dot(x, y, dims):
    return lax.dot_general(x, y, dims, preferred_element_type=jnp.float32)


def kernel(A, Z, B, CB, NX, sizes, left, right, metric, pair, amp, out,
           gathered, send1, got1, own, chip, got2, right_fit, fit, amps, ladder, acc,
           keep, part, got_z, mine, got_ab,
           z_send, z_recv, s_send, s_recv, x_send, x_recv, t_send, t_recv,
           u_send, u_recv, amp_sem, own_sem, fz_send, fz_recv, fa_send, fa_recv):
    aux, z, y = lax.axis_index("aux"), lax.axis_index("cd"), lax.axis_index("ab")
    C, PW = left.shape
    D = right.shape[0]
    Q = metric.shape[1]
    I = amp.shape[0]
    T = pair.shape[0]
    NC = C // CB
    H = D // 2
    HX = H // NX
    QB = min(512, Q)
    core = lax.rem(aux, 2)
    sibling = aux + 1 - 2 * core

    def rcopy(src, dst, ss, rs, dev):
        return pltpu.make_async_remote_copy(src_ref=src, dst_ref=dst, send_sem=ss, recv_sem=rs,
                                            device_id=dev, device_id_type=MESH)

    def plane_peer(o):
        flat = lax.rem(aux * B + y + o, A * B)
        return {"aux": flat // B, "ab": lax.rem(flat, B)}

    def amp_copy(k, slot):
        rows = pl.ds(pl.multiple_of(k * CB, CB), CB)
        return pltpu.make_async_copy(amp.at[:, rows, :], amps.at[slot], amp_sem.at[slot])

    barrier = pltpu.get_barrier_semaphore()
    for o in range(1, Z):
        pl.semaphore_signal(barrier, inc=1, device_id={"cd": lax.rem(z + o, Z)}, device_id_type=MESH)
    for o in range(1, A * B):
        pl.semaphore_signal(barrier, inc=1, device_id=plane_peer(o), device_id_type=MESH)
    pl.semaphore_wait(barrier, Z - 1 + A * B - 1)

    def chunk(k):
        return pl.ds(pl.multiple_of(k * CB, CB), CB)

    def push(src, o, k, way):
        dev = {"cd": z + 1} if way == 0 else {"cd": z - 1}
        return rcopy(src, gathered.at[o, chunk(k)], z_send.at[way, o, k], z_recv.at[o, k], dev)

    def first(k, c):
        @pl.when(z < Z - 1)
        def _():
            push(left.at[chunk(k)], z, k, 0).start()

        @pl.when(z > 0)
        def _():
            push(left.at[chunk(k)], z, k, 1).start()
        return c

    lax.fori_loop(0, NC, first, 0)
    own_copy = pltpu.make_async_copy(left, gathered.at[z], own_sem)
    own_copy.start()
    amp_copy(0, 0).start()
    if NC > 1:
        amp_copy(1, 1).start()

    def relay_chunk(h, k):
        @pl.when(z - h >= 0)
        def _():
            o = z - h
            push(gathered.at[o, chunk(k)], o, k, 0).wait_recv()
            if h < Z - 1:
                @pl.when(z < Z - 1)
                def _():
                    push(gathered.at[o, chunk(k)], o, k, 0).start()

        @pl.when(z + h < Z)
        def _():
            o = z + h
            push(gathered.at[o, chunk(k)], o, k, 1).wait_recv()
            if h < Z - 1:
                @pl.when(z > 0)
                def _():
                    push(gathered.at[o, chunk(k)], o, k, 1).start()

    mine_rows = pl.ds(pl.multiple_of(core * H, H), H)
    other_rows = pl.ds(pl.multiple_of((1 - core) * H, H), H)

    def cols(j):
        return pl.ds(pl.multiple_of(j * QB, QB), QB)

    def fit_other(j, c):
        send1[:, cols(j)] = dot(right[other_rows, :], metric[:, cols(j)], NN).astype(jnp.bfloat16)
        return c

    lax.fori_loop(0, Q // QB, fit_other, 0)

    def block(i):
        return pl.ds(i * HX, HX)

    pair_copies = [rcopy(send1.at[block(i)], got1.at[block(i)], s_send.at[i], s_recv.at[i], {"aux": sibling})
                   for i in range(NX)]
    for cp in pair_copies:
        cp.start()

    def fit_own(j, c):
        own[:, cols(j)] = dot(right[mine_rows, :], metric[:, cols(j)], NN)
        return c

    lax.fori_loop(0, Q // QB, fit_own, 0)
    x_copies = []
    for i in range(NX):
        pair_copies[i].wait()

        def add_pair(j, c, i=i):
            total = own[block(i), cols(j)] + got1[block(i), cols(j)].astype(jnp.float32)
            own[block(i), cols(j)] = total
            chip[block(i), cols(j)] = total.astype(jnp.bfloat16)
            return c

        lax.fori_loop(0, Q // QB, add_pair, 0)
        x_copies.append([rcopy(chip.at[block(i)], got2.at[n, block(i)], x_send.at[n, i], x_recv.at[n, i],
                               {"aux": lax.rem(aux + 2 * n + 2, A)}) for n in range(A // 2 - 1)])
        for cp in x_copies[i]:
            cp.start()

    rows_at = y * C + lax.broadcasted_iota(jnp.int32, (C, T), 0)
    rows_tile = lax.broadcasted_iota(jnp.int32, (C, T), 1)
    cols_at = z * D + lax.broadcasted_iota(jnp.int32, (T, D), 1)
    cols_tile = lax.broadcasted_iota(jnp.int32, (T, D), 0)
    row_hot = jnp.zeros((C, T), jnp.float32)
    col_hot = jnp.zeros((T, D), jnp.float32)
    low = jnp.int32(0)
    for t in range(T):
        high = low + sizes[t]
        row_hot = jnp.where((rows_tile == t) & (rows_at >= low) & (rows_at < high), 1.0, row_hot)
        col_hot = jnp.where((cols_tile == t) & (cols_at >= low) & (cols_at < high), 1.0, col_hot)
        low = high
    pair_bf = pair[...].astype(jnp.float32).astype(jnp.bfloat16)
    hot_rows = dot(row_hot.astype(jnp.bfloat16), pair_bf, NN).astype(jnp.bfloat16)
    keep[...] = dot(hot_rows, col_hot.astype(jnp.bfloat16), NN)
    acc[...] = jnp.zeros_like(acc)
    part[...] = jnp.zeros_like(part)

    def t_copy(i):
        return rcopy(right_fit.at[i, core], right_fit.at[i, core], t_send.at[i], t_recv.at[i], {"aux": sibling})

    def u_rows(i, half):
        return pl.ds(pl.multiple_of(half * H + i * HX, HX), HX)

    def u_copy(i, half, o, owner):
        place = fit.at[owner, u_rows(i, half)]
        return rcopy(place, place, u_send.at[i, half, o - 1], u_recv.at[i, half, o - 1], {"ab": lax.rem(y + o, B)})

    def finish_fit(i):
        t_copy(i).wait()

        def step(j, c):
            keys = pl.ds(pl.multiple_of(j * 256, 256), 256)
            both = dot(right_fit[i].reshape(4 * HX, Q), metric[keys, :], NT).reshape(2, 2, HX, 256)
            both = (both[:, 0] + both[:, 1]).astype(jnp.bfloat16)
            for half in range(2):
                fit[y, u_rows(i, half), keys] = both[half]
            return c

        lax.fori_loop(0, PW // 256, step, 0)
        for o in range(1, B):
            for half in range(2):
                u_copy(i, half, o, y).start()

    for i in range(NX):
        if Z > 2:
            for k in range(i * NC // NX, (i + 1) * NC // NX):
                relay_chunk(1, k)
        for cp in x_copies[i]:
            cp.wait()

        def total_t(j, c, i=i):
            total = own[block(i), cols(j)]
            for n in range(A // 2 - 1):
                total = total + got2[n, block(i), cols(j)].astype(jnp.float32)
            hi = total.astype(jnp.bfloat16)
            right_fit[i, core, 0, :, cols(j)] = hi
            right_fit[i, core, 1, :, cols(j)] = (total - hi.astype(jnp.float32)).astype(jnp.bfloat16)
            return c

        lax.fori_loop(0, Q // QB, total_t, 0)
        t_copy(i).start()
        if i > 0:
            finish_fit(i - 1)
    finish_fit(NX - 1)
    own_copy.wait()
    for i in range(NX):
        for o in range(1, B):
            for half in range(2):
                u_copy(i, half, o, y).wait_send()
                u_copy(i, half, o, lax.rem(y - o + B, B)).wait_recv()

    WIDE = min(2, NC)

    def ladder_rows(o, k, chunks):
        rows = pl.ds(pl.multiple_of(k * CB, CB), chunks * CB)
        groups = pl.ds(k * (CB // GROUP), chunks * CB // GROUP)

        @pl.when((o >= 0) & (o < Z))
        def _():
            kept = keep[rows, :]
            for b in range(B):
                terms = dot(gathered[o, rows, :], fit[b], NT) * kept
                hi = terms.astype(jnp.bfloat16)
                lo = (terms - hi.astype(jnp.float32)).astype(jnp.bfloat16)
                ladder[groups, b, 0, o] = hi.reshape(-1, GROUP, D)
                ladder[groups, b, 1, o] = lo.reshape(-1, GROUP, D)

    def relay_wide(h, k):
        for n in range(WIDE):
            relay_chunk(h, k * WIDE + n)

    def near(k, c):
        ladder_rows(z, k * WIDE, WIDE)
        if Z > 2:
            ladder_rows(z - 1, k * WIDE, WIDE)
            ladder_rows(z + 1, k * WIDE, WIDE)
        if Z > 3:
            relay_wide(2, k)
        return c

    lax.fori_loop(0, NC // WIDE, near, 0)
    for h in range(2, Z - 1):
        def far(k, c, h=h):
            if h > 2:
                relay_wide(h, k)
            ladder_rows(z - h, k * WIDE, WIDE)
            ladder_rows(z + h, k * WIDE, WIDE)
            return c
        lax.fori_loop(0, NC // WIDE, far, 0)

    NR = B * 2 * Z * GROUP
    NG = CB // GROUP
    NB = min(NR, 256)

    def ladder_chunk(k, carry):
        slot = lax.rem(k, 2)
        relay_chunk(Z - 1, k)
        if Z > 1:
            ladder_rows(z - (Z - 1), k, 1)
            ladder_rows(z + (Z - 1), k, 1)
        amp_copy(k, slot).wait()

        def contract(g, c):
            kept = amps[slot, :, pl.ds(pl.multiple_of(g * GROUP, GROUP), GROUP), :].reshape(I * GROUP, D)
            flat = ladder[k * NG + g].reshape(NR, D)
            for n in range(0, NR, NB):
                acc[:, n:n + NB] += dot(kept, flat[n:n + NB], NT)
            return c

        lax.fori_loop(0, NG, contract, 0)

        @pl.when(k + 2 < NC)
        def _():
            amp_copy(k + 2, slot).start()
        return carry

    lax.fori_loop(0, NC, ladder_chunk, 0)

    total = acc[...]
    same = (lax.rem(lax.broadcasted_iota(jnp.int32, total.shape, 0), GROUP)
            == lax.rem(lax.broadcasted_iota(jnp.int32, total.shape, 1), GROUP))
    total = jnp.sum(jnp.where(same, total, 0.0).reshape(I, GROUP, NR), axis=1)
    pick_row = lax.broadcasted_iota(jnp.int32, (Z * 8, NR), 0)
    pick_col = lax.broadcasted_iota(jnp.int32, (Z * 8, NR), 1)
    want = lax.rem(lax.div(pick_col, GROUP), Z) * 8 + lax.div(pick_col, 2 * Z * GROUP)
    pick = jnp.where(pick_row == want, 1.0, 0.0)
    sums = lax.dot_general(pick, total, NT, precision=lax.Precision.HIGHEST,
                           preferred_element_type=jnp.float32)
    part[:, :, :I] = sums.reshape(Z, 8, I)

    def fz(o):
        dest = lax.rem(z + o, Z)
        return rcopy(part.at[dest], got_z.at[o - 1], fz_send.at[o - 1], fz_recv.at[o - 1], {"cd": dest})

    for o in range(1, Z):
        fz(o).start()
    summed = part[z]
    for o in range(1, Z):
        fz(o).wait()
        summed = summed + got_z[o - 1]
    mine[...] = summed

    def fa(o):
        return rcopy(mine, got_ab.at[o - 1], fa_send.at[o - 1], fa_recv.at[o - 1], plane_peer(o))

    for o in range(1, A * B):
        fa(o).start()
    for o in range(1, A * B):
        fa(o).wait()
        summed = summed + got_ab[o - 1]
    row = lax.broadcasted_iota(jnp.int32, summed.shape, 0)
    out[...] = jnp.sum(jnp.where(row == y, summed, 0.0), axis=0, keepdims=True)[:, :I]

    for h in range(0, Z - 1):
        for way in (0, 1):
            o = z - h if way == 0 else z + h
            ok = (z - h >= 0) & (z < Z - 1) if way == 0 else (z + h < Z) & (z > 0)

            def drain(k, c, o=o, way=way, ok=ok):
                @pl.when(ok)
                def _():
                    push(gathered.at[o, chunk(k)], o, k, way).wait_send()
                return c
            lax.fori_loop(0, NC, drain, 0)


def body(left, right, metric, amplitudes, sizes, pair):
    A, Z, B = lax.axis_size("aux"), lax.axis_size("cd"), lax.axis_size("ab")
    a_local, C, PW = left.shape
    b_local, D, _ = right.shape
    Q = metric.shape[1]
    I = amplitudes.shape[0]
    T = pair.shape[0]
    CB = min(128, C)
    NC = C // CB
    H = D // 2
    NX = min(4, NC)
    NR = B * 2 * Z * GROUP
    X = max(A // 2 - 1, 1)
    bf, f32 = jnp.bfloat16, jnp.float32
    dma = pltpu.SemaphoreType.DMA
    vmem = pl.BlockSpec(memory_space=pltpu.VMEM)
    out = pl.pallas_call(
        functools.partial(kernel, A, Z, B, CB, NX),
        out_shape=jax.ShapeDtypeStruct((1, I), f32),
        in_specs=[pl.BlockSpec(memory_space=pltpu.SMEM), vmem, vmem, vmem, vmem,
                  pl.BlockSpec(memory_space=pl.ANY)],
        out_specs=vmem,
        scratch_shapes=[
            pltpu.VMEM((Z, C, PW), bf),
            pltpu.VMEM((H, Q), bf), pltpu.VMEM((H, Q), bf), pltpu.VMEM((H, Q), f32),
            pltpu.VMEM((H, Q), bf), pltpu.VMEM((X, H, Q), bf),
            pltpu.VMEM((NX, 2, 2, H // NX, Q), bf),
            pltpu.VMEM((B, D, PW), bf),
            pltpu.VMEM((2, I, CB, D), bf),
            pltpu.VMEM((C // GROUP, B, 2, Z, GROUP, D), bf),
            pltpu.VMEM((I * GROUP, NR), f32),
            pltpu.VMEM((C, D), f32),
            pltpu.VMEM((Z, 8, 128), f32), pltpu.VMEM((max(Z - 1, 1), 8, 128), f32),
            pltpu.VMEM((8, 128), f32), pltpu.VMEM((max(A * B - 1, 1), 8, 128), f32),
            dma((2, Z, NC)), dma((Z, NC)), dma((NX,)), dma((NX,)), dma((X, NX)), dma((X, NX)), dma((NX,)), dma((NX,)),
            dma((NX, 2, max(B - 1, 1))), dma((NX, 2, max(B - 1, 1))), dma((2,)), dma,
            dma((max(Z - 1, 1),)), dma((max(Z - 1, 1),)),
            dma((max(A * B - 1, 1),)), dma((max(A * B - 1, 1),)),
        ],
        compiler_params=pltpu.CompilerParams(collective_id=0, has_side_effects=True,
                                             vmem_limit_bytes=60 * 1024 * 1024),
        name="ladder",
    )(sizes, left.reshape(C, PW), right.reshape(D, PW), metric, pair, amplitudes)
    return out.reshape(a_local, b_local, I)


def solution(mesh):
    return jax.shard_map(
        body,
        mesh=mesh,
        in_specs=(
            P("cd", "ab", "aux"),
            P("ab", "cd", "aux"),
            P("aux", None),
            P(None, "ab", "cd"),
            P(),
            P(),
        ),
        out_specs=P("cd", "ab", None),
        check_vma=False,
    )
```

```python
import functools

import jax
import jax.numpy as jnp
from jax import lax
from jax.experimental import pallas as pl
from jax.experimental.pallas import tpu as pltpu
from jax.sharding import PartitionSpec as P

NT = (((1,), (1,)), ((), ()))
NN = (((1,), (0,)), ((), ()))
GROUP = 16
MESH = pl.DeviceIdType.MESH


def dot(x, y, dims):
    return lax.dot_general(x, y, dims, preferred_element_type=jnp.float32)


def kernel(A, Z, B, CB, NX, sizes, left, right, metric, pair, amp, out,
           gathered, send1, got1, own, chip, got2, right_fit, fit, amps, ladder, acc,
           keep, part, got_z, mine, got_ab,
           z_send, z_recv, s_send, s_recv, x_send, x_recv, t_send, t_recv,
           u_send, u_recv, amp_sem, own_sem, fz_send, fz_recv, fa_send, fa_recv):
    aux, z, y = lax.axis_index("aux"), lax.axis_index("cd"), lax.axis_index("ab")
    C, PW = left.shape
    D = right.shape[0]
    Q = metric.shape[1]
    I = amp.shape[0]
    T = pair.shape[0]
    NC = C // CB
    H = D // 2
    HX = H // NX
    QB = min(512, Q)
    core = lax.rem(aux, 2)
    sibling = aux + 1 - 2 * core

    def rcopy(src, dst, ss, rs, dev):
        return pltpu.make_async_remote_copy(src_ref=src, dst_ref=dst, send_sem=ss, recv_sem=rs,
                                            device_id=dev, device_id_type=MESH)

    def plane_peer(o):
        flat = lax.rem(aux * B + y + o, A * B)
        return {"aux": flat // B, "ab": lax.rem(flat, B)}

    def amp_copy(k, slot):
        rows = pl.ds(pl.multiple_of(k * CB, CB), CB)
        return pltpu.make_async_copy(amp.at[:, rows, :], amps.at[slot], amp_sem.at[slot])

    barrier = pltpu.get_barrier_semaphore()
    for o in range(1, Z):
        pl.semaphore_signal(barrier, inc=1, device_id={"cd": lax.rem(z + o, Z)}, device_id_type=MESH)
    for o in range(1, A * B):
        pl.semaphore_signal(barrier, inc=1, device_id=plane_peer(o), device_id_type=MESH)
    pl.semaphore_wait(barrier, Z - 1 + A * B - 1)

    def chunk(k):
        return pl.ds(pl.multiple_of(k * CB, CB), CB)

    def push(src, o, k, way):
        dev = {"cd": z + 1} if way == 0 else {"cd": z - 1}
        return rcopy(src, gathered.at[o, chunk(k)], z_send.at[way, o, k], z_recv.at[o, k], dev)

    def first(k, c):
        @pl.when(z < Z - 1)
        def _():
            push(left.at[chunk(k)], z, k, 0).start()

        @pl.when(z > 0)
        def _():
            push(left.at[chunk(k)], z, k, 1).start()
        return c

    lax.fori_loop(0, NC, first, 0)
    own_copy = pltpu.make_async_copy(left, gathered.at[z], own_sem)
    own_copy.start()
    amp_copy(0, 0).start()
    if NC > 1:
        amp_copy(1, 1).start()

    def relay_chunk(h, k):
        @pl.when(z - h >= 0)
        def _():
            o = z - h
            push(gathered.at[o, chunk(k)], o, k, 0).wait_recv()
            if h < Z - 1:
                @pl.when(z < Z - 1)
                def _():
                    push(gathered.at[o, chunk(k)], o, k, 0).start()

        @pl.when(z + h < Z)
        def _():
            o = z + h
            push(gathered.at[o, chunk(k)], o, k, 1).wait_recv()
            if h < Z - 1:
                @pl.when(z > 0)
                def _():
                    push(gathered.at[o, chunk(k)], o, k, 1).start()

    mine_rows = pl.ds(pl.multiple_of(core * H, H), H)
    other_rows = pl.ds(pl.multiple_of((1 - core) * H, H), H)

    def cols(j):
        return pl.ds(pl.multiple_of(j * QB, QB), QB)

    def fit_other(j, c):
        send1[:, cols(j)] = dot(right[other_rows, :], metric[:, cols(j)], NN).astype(jnp.bfloat16)
        return c

    lax.fori_loop(0, Q // QB, fit_other, 0)

    def block(i):
        return pl.ds(i * HX, HX)

    pair_copies = [rcopy(send1.at[block(i)], got1.at[block(i)], s_send.at[i], s_recv.at[i], {"aux": sibling})
                   for i in range(NX)]
    for cp in pair_copies:
        cp.start()

    def fit_own(j, c):
        own[:, cols(j)] = dot(right[mine_rows, :], metric[:, cols(j)], NN)
        return c

    lax.fori_loop(0, Q // QB, fit_own, 0)
    x_copies = []
    for i in range(NX):
        pair_copies[i].wait()

        def add_pair(j, c, i=i):
            total = own[block(i), cols(j)] + got1[block(i), cols(j)].astype(jnp.float32)
            own[block(i), cols(j)] = total
            chip[block(i), cols(j)] = total.astype(jnp.bfloat16)
            return c

        lax.fori_loop(0, Q // QB, add_pair, 0)
        x_copies.append([rcopy(chip.at[block(i)], got2.at[n, block(i)], x_send.at[n, i], x_recv.at[n, i],
                               {"aux": lax.rem(aux + 2 * n + 2, A)}) for n in range(A // 2 - 1)])
        for cp in x_copies[i]:
            cp.start()

    rows_at = y * C + lax.broadcasted_iota(jnp.int32, (C, T), 0)
    rows_tile = lax.broadcasted_iota(jnp.int32, (C, T), 1)
    cols_at = z * D + lax.broadcasted_iota(jnp.int32, (T, D), 1)
    cols_tile = lax.broadcasted_iota(jnp.int32, (T, D), 0)
    row_hot = jnp.zeros((C, T), jnp.float32)
    col_hot = jnp.zeros((T, D), jnp.float32)
    low = jnp.int32(0)
    for t in range(T):
        high = low + sizes[t]
        row_hot = jnp.where((rows_tile == t) & (rows_at >= low) & (rows_at < high), 1.0, row_hot)
        col_hot = jnp.where((cols_tile == t) & (cols_at >= low) & (cols_at < high), 1.0, col_hot)
        low = high
    pair_bf = pair[...].astype(jnp.float32).astype(jnp.bfloat16)
    hot_rows = dot(row_hot.astype(jnp.bfloat16), pair_bf, NN).astype(jnp.bfloat16)
    keep[...] = dot(hot_rows, col_hot.astype(jnp.bfloat16), NN)
    acc[...] = jnp.zeros_like(acc)
    part[...] = jnp.zeros_like(part)

    def t_copy(i):
        return rcopy(right_fit.at[i, core], right_fit.at[i, core], t_send.at[i], t_recv.at[i], {"aux": sibling})

    def u_rows(i, half):
        return pl.ds(pl.multiple_of(half * H + i * HX, HX), HX)

    def u_copy(i, half, o, owner):
        place = fit.at[owner, u_rows(i, half)]
        return rcopy(place, place, u_send.at[i, half, o - 1], u_recv.at[i, half, o - 1], {"ab": lax.rem(y + o, B)})

    def finish_fit(i):
        t_copy(i).wait()

        def step(j, c):
            keys = pl.ds(pl.multiple_of(j * 256, 256), 256)
            both = dot(right_fit[i].reshape(4 * HX, Q), metric[keys, :], NT).reshape(2, 2, HX, 256)
            both = (both[:, 0] + both[:, 1]).astype(jnp.bfloat16)
            for half in range(2):
                fit[y, u_rows(i, half), keys] = both[half]
            return c

        lax.fori_loop(0, PW // 256, step, 0)
        for o in range(1, B):
            for half in range(2):
                u_copy(i, half, o, y).start()

    for i in range(NX):
        if Z > 2:
            for k in range(i * NC // NX, (i + 1) * NC // NX):
                relay_chunk(1, k)
        for cp in x_copies[i]:
            cp.wait()

        def total_t(j, c, i=i):
            total = own[block(i), cols(j)]
            for n in range(A // 2 - 1):
                total = total + got2[n, block(i), cols(j)].astype(jnp.float32)
            hi = total.astype(jnp.bfloat16)
            right_fit[i, core, 0, :, cols(j)] = hi
            right_fit[i, core, 1, :, cols(j)] = (total - hi.astype(jnp.float32)).astype(jnp.bfloat16)
            return c

        lax.fori_loop(0, Q // QB, total_t, 0)
        t_copy(i).start()
        if i > 0:
            finish_fit(i - 1)
    finish_fit(NX - 1)
    own_copy.wait()
    for i in range(NX):
        for o in range(1, B):
            for half in range(2):
                u_copy(i, half, o, y).wait_send()
                u_copy(i, half, o, lax.rem(y - o + B, B)).wait_recv()

    WIDE = min(2, NC)

    def ladder_rows(o, k, chunks):
        rows = pl.ds(pl.multiple_of(k * CB, CB), chunks * CB)
        groups = pl.ds(k * (CB // GROUP), chunks * CB // GROUP)

        @pl.when((o >= 0) & (o < Z))
        def _():
            kept = keep[rows, :]
            for b in range(B):
                terms = dot(gathered[o, rows, :], fit[b], NT) * kept
                hi = terms.astype(jnp.bfloat16)
                lo = (terms - hi.astype(jnp.float32)).astype(jnp.bfloat16)
                ladder[groups, b, 0, o] = hi.reshape(-1, GROUP, D)
                ladder[groups, b, 1, o] = lo.reshape(-1, GROUP, D)

    def relay_wide(h, k):
        for n in range(WIDE):
            relay_chunk(h, k * WIDE + n)

    def near(k, c):
        if Z > 3:
            relay_wide(2, k)
        ladder_rows(z, k * WIDE, WIDE)
        if Z > 2:
            ladder_rows(z - 1, k * WIDE, WIDE)
            ladder_rows(z + 1, k * WIDE, WIDE)
        return c

    lax.fori_loop(0, NC // WIDE, near, 0)
    for h in range(2, Z - 1):
        def far(k, c, h=h):
            if h > 2:
                relay_wide(h, k)
            ladder_rows(z - h, k * WIDE, WIDE)
            ladder_rows(z + h, k * WIDE, WIDE)
            return c
        lax.fori_loop(0, NC // WIDE, far, 0)

    NR = B * 2 * Z * GROUP
    NG = CB // GROUP
    NB = min(NR, 256)

    def ladder_chunk(k, carry):
        slot = lax.rem(k, 2)
        relay_chunk(Z - 1, k)
        if Z > 1:
            ladder_rows(z - (Z - 1), k, 1)
            ladder_rows(z + (Z - 1), k, 1)
        amp_copy(k, slot).wait()

        def contract(g, c):
            kept = amps[slot, :, pl.ds(pl.multiple_of(g * GROUP, GROUP), GROUP), :].reshape(I * GROUP, D)
            flat = ladder[k * NG + g].reshape(NR, D)
            for n in range(0, NR, NB):
                acc[:, n:n + NB] += dot(kept, flat[n:n + NB], NT)
            return c

        lax.fori_loop(0, NG, contract, 0)

        @pl.when(k + 2 < NC)
        def _():
            amp_copy(k + 2, slot).start()
        return carry

    lax.fori_loop(0, NC, ladder_chunk, 0)

    total = acc[...]
    same = (lax.rem(lax.broadcasted_iota(jnp.int32, total.shape, 0), GROUP)
            == lax.rem(lax.broadcasted_iota(jnp.int32, total.shape, 1), GROUP))
    total = jnp.sum(jnp.where(same, total, 0.0).reshape(I, GROUP, NR), axis=1)
    pick_row = lax.broadcasted_iota(jnp.int32, (Z * 8, NR), 0)
    pick_col = lax.broadcasted_iota(jnp.int32, (Z * 8, NR), 1)
    want = lax.rem(lax.div(pick_col, GROUP), Z) * 8 + lax.div(pick_col, 2 * Z * GROUP)
    pick = jnp.where(pick_row == want, 1.0, 0.0)
    sums = lax.dot_general(pick, total, NT, precision=lax.Precision.HIGHEST,
                           preferred_element_type=jnp.float32)
    part[:, :, :I] = sums.reshape(Z, 8, I)

    def fz(o):
        dest = lax.rem(z + o, Z)
        return rcopy(part.at[dest], got_z.at[o - 1], fz_send.at[o - 1], fz_recv.at[o - 1], {"cd": dest})

    for o in range(1, Z):
        fz(o).start()
    summed = part[z]
    for o in range(1, Z):
        fz(o).wait()
        summed = summed + got_z[o - 1]
    mine[...] = summed

    def fa(o):
        return rcopy(mine, got_ab.at[o - 1], fa_send.at[o - 1], fa_recv.at[o - 1], plane_peer(o))

    for o in range(1, A * B):
        fa(o).start()
    for o in range(1, A * B):
        fa(o).wait()
        summed = summed + got_ab[o - 1]
    row = lax.broadcasted_iota(jnp.int32, summed.shape, 0)
    out[...] = jnp.sum(jnp.where(row == y, summed, 0.0), axis=0, keepdims=True)[:, :I]

    for h in range(0, Z - 1):
        for way in (0, 1):
            o = z - h if way == 0 else z + h
            ok = (z - h >= 0) & (z < Z - 1) if way == 0 else (z + h < Z) & (z > 0)

            def drain(k, c, o=o, way=way, ok=ok):
                @pl.when(ok)
                def _():
                    push(gathered.at[o, chunk(k)], o, k, way).wait_send()
                return c
            lax.fori_loop(0, NC, drain, 0)


def body(left, right, metric, amplitudes, sizes, pair):
    A, Z, B = lax.axis_size("aux"), lax.axis_size("cd"), lax.axis_size("ab")
    a_local, C, PW = left.shape
    b_local, D, _ = right.shape
    Q = metric.shape[1]
    I = amplitudes.shape[0]
    T = pair.shape[0]
    CB = min(128, C)
    NC = C // CB
    H = D // 2
    NX = min(4, NC)
    NR = B * 2 * Z * GROUP
    X = max(A // 2 - 1, 1)
    bf, f32 = jnp.bfloat16, jnp.float32
    dma = pltpu.SemaphoreType.DMA
    vmem = pl.BlockSpec(memory_space=pltpu.VMEM)
    out = pl.pallas_call(
        functools.partial(kernel, A, Z, B, CB, NX),
        out_shape=jax.ShapeDtypeStruct((1, I), f32),
        in_specs=[pl.BlockSpec(memory_space=pltpu.SMEM), vmem, vmem, vmem, vmem,
                  pl.BlockSpec(memory_space=pl.ANY)],
        out_specs=vmem,
        scratch_shapes=[
            pltpu.VMEM((Z, C, PW), bf),
            pltpu.VMEM((H, Q), bf), pltpu.VMEM((H, Q), bf), pltpu.VMEM((H, Q), f32),
            pltpu.VMEM((H, Q), bf), pltpu.VMEM((X, H, Q), bf),
            pltpu.VMEM((NX, 2, 2, H // NX, Q), bf),
            pltpu.VMEM((B, D, PW), bf),
            pltpu.VMEM((2, I, CB, D), bf),
            pltpu.VMEM((C // GROUP, B, 2, Z, GROUP, D), bf),
            pltpu.VMEM((I * GROUP, NR), f32),
            pltpu.VMEM((C, D), f32),
            pltpu.VMEM((Z, 8, 128), f32), pltpu.VMEM((max(Z - 1, 1), 8, 128), f32),
            pltpu.VMEM((8, 128), f32), pltpu.VMEM((max(A * B - 1, 1), 8, 128), f32),
            dma((2, Z, NC)), dma((Z, NC)), dma((NX,)), dma((NX,)), dma((X, NX)), dma((X, NX)), dma((NX,)), dma((NX,)),
            dma((NX, 2, max(B - 1, 1))), dma((NX, 2, max(B - 1, 1))), dma((2,)), dma,
            dma((max(Z - 1, 1),)), dma((max(Z - 1, 1),)),
            dma((max(A * B - 1, 1),)), dma((max(A * B - 1, 1),)),
        ],
        compiler_params=pltpu.CompilerParams(collective_id=0, has_side_effects=True,
                                             vmem_limit_bytes=60 * 1024 * 1024),
        name="ladder",
    )(sizes, left.reshape(C, PW), right.reshape(D, PW), metric, pair, amplitudes)
    return out.reshape(a_local, b_local, I)


def solution(mesh):
    return jax.shard_map(
        body,
        mesh=mesh,
        in_specs=(
            P("cd", "ab", "aux"),
            P("ab", "cd", "aux"),
            P("aux", None),
            P(None, "ab", "cd"),
            P(),
            P(),
        ),
        out_specs=P("cd", "ab", None),
        check_vma=False,
    )
```
